32 devices in a mesh: row: 16 (over z, y, core), col: 2 (over x).
Axes of the slice: x: 2, y: 2, z: 4, core: 2. Of those that a mesh axis runs over, the one named last changes fastest.
Arguments:
- residues: int32 [512], P('row'), may hold values from 0 to 20
- embed_table: bfloat16 [21, 256], replicated, may hold values from -6 to 6
- conv_first: bfloat16 [4352, 256], replicated, may hold values from -0.09375 to 0.09375
- conv_second: bfloat16 [4352, 256], replicated, may hold values from -0.09375 to 0.09375
- proj_row: bfloat16 [256, 64], replicated, may hold values from -0.375 to 0.375
- proj_col: bfloat16 [256, 64], replicated, may hold values from -0.375 to 0.375
- pair_weights: bfloat16 [4, 64, 576], replicated, may hold values from -0.25 to 0.25
Outputs:
- pair_out: bfloat16 [64, 512, 512], P(None, 'row', 'col')
The draws below stay inside these ranges and needn't reach their ends.
All inputs are finite; a program needn't handle non-finite values.
Results may differ from the reference program's by a relative error of at most 0.018.
Values may be sent and summed in bfloat16 or wider, within the bound.
A program may use at most 64 MiB of HBM per device.

```python
import jax
import jax.numpy as jnp
from jax import lax

W = 256
C = 64
VOCAB = 21
KERNEL = 17
LAYERS = 4
WINDOW = 512


def place_ends(entries, key, smallest, high):
    index_at = [jax.random.randint(jax.random.fold_in(key, axis), (), 0, length) for axis, length in enumerate(entries.shape)]
    main_axis = entries.shape.index(max(entries.shape))
    neighbour = index_at[:main_axis] + [(index_at[main_axis] + 1) % entries.shape[main_axis]] + index_at[main_axis + 1:]
    return entries.at[tuple(index_at)].set(smallest).at[tuple(neighbour)].set(high)


def scatter_about(stream_key, dims, scale, reach, kind=jnp.bfloat16):
    entries = jax.random.normal(stream_key, dims, jnp.float32) * scale
    return jnp.minimum(jnp.maximum(entries, -reach), reach).astype(kind)


def setup_inputs(seed: int = 0) -> dict:
    key_of = jax.random.split(jax.random.key(seed), 8)
    return {
        "residues": place_ends(jax.random.randint(key_of[0], (WINDOW,), 0, VOCAB), jax.random.fold_in(key_of[0], 1), 0, VOCAB - 1).astype(jnp.int32),
        "embed_table": scatter_about(key_of[1], (VOCAB, W), 1.0, 6.0),
        "conv_first": scatter_about(key_of[2], (KERNEL * W, W), (KERNEL * W) ** -0.5, 0.09375),
        "conv_second": scatter_about(key_of[3], (KERNEL * W, W), (KERNEL * W) ** -0.5, 0.09375),
        "proj_row": scatter_about(key_of[4], (W, C), W ** -0.5, 0.375),
        "proj_col": scatter_about(key_of[5], (W, C), W ** -0.5, 0.375),
        "pair_weights": scatter_about(key_of[6], (LAYERS, C, 9 * C), (9 * C) ** -0.5, 0.25),
    }


def elu(v):
    return jnp.where(v > 0, v, jnp.expm1(jnp.minimum(v, 0.0)))


def conv_seq(feats, weight_stack):
    half = KERNEL // 2
    length = feats.shape[0]
    padded = jnp.pad(feats, ((half, half), (0, 0)))
    windows = jnp.concatenate([padded[k:k + length] for k in range(KERNEL)], axis=1)
    return jnp.dot(windows, weight_stack, preferred_element_type=jnp.float32)


def reference(residues, embed_table, conv_first, conv_second, proj_row, proj_col, pair_weights):
    onehot = (residues[:, None] == jnp.arange(VOCAB, dtype=jnp.int32)[None, :]).astype(jnp.bfloat16)
    embedded = jnp.dot(onehot, embed_table, preferred_element_type=jnp.float32).astype(jnp.bfloat16)
    first = elu(conv_seq(embedded, conv_first)).astype(jnp.bfloat16)
    second = (first.astype(jnp.float32) + elu(conv_seq(first, conv_second))).astype(jnp.bfloat16)
    left = jnp.dot(second, proj_row, preferred_element_type=jnp.float32).astype(jnp.bfloat16)
    right = jnp.dot(second, proj_col, preferred_element_type=jnp.float32).astype(jnp.bfloat16)
    pair_features = (left.T.astype(jnp.float32)[:, :, None] + right.T.astype(jnp.float32)[:, None, :]).astype(jnp.bfloat16)
    for layer_number in range(LAYERS):
        dilation_rate = 2 ** layer_number
        activation_map = elu(pair_features.astype(jnp.float32)).astype(jnp.bfloat16).astype(jnp.float32)
        filter_kernel = pair_weights[layer_number].astype(jnp.float32).reshape(C, 3, 3, C).transpose(0, 3, 1, 2)
        output_map = lax.conv_general_dilated(activation_map[None], filter_kernel, (1, 1), ((dilation_rate, dilation_rate), (dilation_rate, dilation_rate)), rhs_dilation=(dilation_rate, dilation_rate), dimension_numbers=("NCHW", "OIHW", "NCHW"), precision=lax.Precision.HIGHEST)[0]
        pair_features = (pair_features.astype(jnp.float32) + output_map).astype(jnp.bfloat16)
    return pair_features
```

```python
import functools

import jax
import jax.numpy as jnp
from jax import lax
from jax.experimental import pallas as pl
from jax.experimental.pallas import tpu as pltpu
from jax.sharding import PartitionSpec as P

MESH = pl.DeviceIdType.MESH
HALO = 16
F32, BF16 = jnp.float32, jnp.bfloat16


def gather_kernel(n, res_ref, out_ref, buf, send_sem, recv_sem):
    me = lax.axis_index("row")
    barrier = pltpu.get_barrier_semaphore()
    for s in range(1, n):
        pl.semaphore_signal(
            barrier, inc=1, device_id={"row": lax.rem(me + s, n)}, device_id_type=MESH
        )
    pl.semaphore_wait(barrier, n - 1)
    copies = []
    for s in range(1, n):
        copy = pltpu.make_async_remote_copy(
            src_ref=res_ref,
            dst_ref=buf.at[me],
            send_sem=send_sem.at[s],
            recv_sem=recv_sem.at[s],
            device_id={"row": lax.rem(me + s, n)},
            device_id_type=MESH,
        )
        copy.start()
        copies.append(copy)
    for copy in copies:
        copy.wait()
    out_ref[...] = buf[...]
    out_ref[me] = res_ref[...]


def gather_residues(residues, n):
    length = residues.shape[0]
    return pl.pallas_call(
        functools.partial(gather_kernel, n),
        out_shape=jax.ShapeDtypeStruct((n, 1, length), jnp.int32),
        in_specs=[pl.BlockSpec(memory_space=pltpu.VMEM)],
        out_specs=pl.BlockSpec(memory_space=pltpu.VMEM),
        scratch_shapes=[
            pltpu.VMEM((n, 1, length), jnp.int32),
            pltpu.SemaphoreType.DMA((n,)),
            pltpu.SemaphoreType.DMA((n,)),
        ],
        compiler_params=pltpu.CompilerParams(collective_id=0, has_side_effects=True),
        name="gather",
    )(residues.reshape(1, length))


def elu(v):
    return jnp.where(v > 0, v, jnp.exp(jnp.minimum(v, 0.0)) - 1.0)


def main_kernel(
    dims, res_ref, table_ref, w1_ref, w2_ref, prow_ref, pcol_ref, pw_ref, out_ref,
    tab, emb, xs, fs, cols, la, lb, right_ref, pair, act_a, act_b, bw,
):
    rows, ncol, span, tile, chans, kernel, layers = dims
    me_r, me_c = lax.axis_index("row"), lax.axis_index("col")
    window = rows * span
    width = table_ref.shape[1]
    half = kernel // 2
    edge = 2 * HALO
    n_row, n_col = span + 2 * edge, tile + 2 * edge
    height, wide = span + 2 * HALO, tile + 2 * HALO
    two = 2 * chans

    zero = jnp.zeros((chans, chans), BF16)
    for layer in range(layers):
        w = pw_ref[layer]
        blk = lambda ty, tx: w[:, (3 * ty + tx) * chans : (3 * ty + tx + 1) * chans]
        for tx in range(3):
            b0, b1, b2 = (blk(ty, tx) for ty in range(3))
            if layer == 0:
                lines = ([b1, b2, zero, b0], [b0, b1, b2, zero])
            else:
                lines = ([b0, zero, b1, zero, b2, zero], [zero, b0, zero, b1, zero, b2])
            for h in range(2):
                row = jnp.concatenate(lines[h], axis=1)
                bw[layer, pl.ds(tx * two + h * chans, chans), 0 : row.shape[1]] = row

    tab[...] = jnp.zeros_like(tab)
    tab[0 : table_ref.shape[0], :] = table_ref[...]
    emb[0:edge, :] = jnp.zeros((edge, width), F32)
    emb[edge + window : 2 * edge + window, :] = jnp.zeros((edge, width), F32)
    per = 128 // span
    vocab = lax.broadcasted_iota(jnp.int32, (tab.shape[0], 128), 0)
    for g in range(window // 128):
        line = jnp.concatenate([res_ref[per * g + m] for m in range(per)], axis=1)
        hot = (jnp.broadcast_to(line, vocab.shape) == vocab).astype(F32).astype(BF16)
        emb[edge + 128 * g : edge + 128 * (g + 1), :] = lax.dot_general(
            hot, tab[...], (((0,), (0,)), ((), ())), preferred_element_type=F32
        )
    xs[0:n_row, :] = emb[pl.ds(pl.multiple_of(me_r * span, span), n_row), :]
    xs[n_row : n_row + n_col, :] = emb[pl.ds(pl.multiple_of(me_c * tile, tile), n_col), :]

    n_first = n_row + n_col - 2 * half
    n_second = n_first - 2 * half
    for k in range(kernel):
        cols[:, k * width : (k + 1) * width] = xs[k : k + n_first, :].astype(BF16)
    first = elu(jnp.dot(cols[...], w1_ref[...], preferred_element_type=F32))
    at = lax.broadcasted_iota(jnp.int32, (n_first, width), 0) + half
    pos = at + jnp.where(at < n_row, me_r * span - edge, me_c * tile - edge - n_row)
    first = jnp.where((pos >= 0) & (pos < window), first, 0.0)
    fs[...] = first.astype(BF16).astype(F32)
    for k in range(kernel):
        cols[0:n_second, k * width : (k + 1) * width] = fs[k : k + n_second, :].astype(BF16)
    second = elu(jnp.dot(cols[0:n_second, :], w2_ref[...], preferred_element_type=F32))
    second = (fs[half : half + n_second, :] + second).astype(BF16)

    blank = jnp.zeros((width, chans), BF16)
    pr, pc = prow_ref[...], pcol_ref[...]
    s_row, s_col = second[0:height], second[n_row : n_row + wide]
    dot = functools.partial(jnp.dot, preferred_element_type=F32)
    la[...] = dot(s_row, jnp.concatenate([pr, blank], axis=1)).astype(BF16).astype(F32)
    lb[...] = dot(s_row, jnp.concatenate([blank, pr], axis=1)).astype(BF16).astype(F32)
    right_ref[...] = dot(s_col, jnp.concatenate([pc, pc], axis=1)).astype(BF16).astype(F32)
    n_pair = height // 2
    blank_pair = jnp.zeros((wide, two), BF16)
    act_a[0] = blank_pair
    act_a[n_pair + 1] = blank_pair

    def mask(act):
        side = jnp.zeros((HALO // 2, wide, two), BF16)
        stripe = jnp.zeros((n_pair + 2, HALO, two), BF16)

        @pl.when(me_r == 0)
        def _():
            act[1 : 1 + HALO // 2] = side

        @pl.when(me_r == rows - 1)
        def _():
            act[1 + n_pair - HALO // 2 : 1 + n_pair] = side

        @pl.when(me_c == 0)
        def _():
            act[:, 0:HALO, :] = stripe

        @pl.when(me_c == ncol - 1)
        def _():
            act[:, wide - HALO : wide, :] = stripe

    def start(p, _):
        left = la[pl.ds(2 * p, 1), :] + lb[pl.ds(2 * p + 1, 1), :]
        value = (right_ref[...] + left).astype(BF16)
        pair[p] = value
        act_a[p + 1] = elu(value.astype(F32)).astype(BF16)
        return 0

    lax.fori_loop(0, n_pair, start, 0)
    mask(act_a)

    lane = lax.broadcasted_iota(jnp.int32, (wide, two), 1)
    bufs = (act_a, act_b)
    reach = 0
    for layer in range(layers):
        src, dst = bufs[layer % 2], bufs[(layer + 1) % 2]
        d = 2**layer
        reach += d
        last = layer == layers - 1
        lo = HALO // 2 if last else reach // 2
        depth = 4 * chans if layer == 0 else 6 * chans

        def step(p, _, layer=layer, src=src, dst=dst, d=d, last=last, depth=depth):
            if layer == 0:
                outer = jnp.where(lane < chans, src[p + 2], src[p])
                lhs = jnp.concatenate([src[p + 1], outer], axis=1)
            else:
                e = d // 2
                lhs = jnp.concatenate([src[p + 1 - e], src[p + 1], src[p + 1 + e]], axis=1)
            got = lax.dot_general(
                lhs, bw[layer, :, 0:depth], (((1,), (1,)), ((), ())), preferred_element_type=F32
            )
            mid = got[:, two : 2 * two]
            low = pltpu.roll(got[:, 0:two], d, 0)
            high = pltpu.roll(got[:, 2 * two : 3 * two], wide - d, 0)
            value = (pair[p].astype(F32) + (low + mid + high)).astype(BF16)
            if last:
                turned = value[HALO : HALO + tile].astype(F32).T.astype(BF16)
                out_ref[2 * (p - HALO // 2)] = turned[0:chans]
                out_ref[2 * (p - HALO // 2) + 1] = turned[chans:two]
            else:
                pair[p] = value
                dst[p + 1] = elu(value.astype(F32)).astype(BF16)
            return 0

        lax.fori_loop(lo, n_pair - lo, step, 0)
        if not last:
            mask(dst)


def local(residues, embed_table, conv_first, conv_second, proj_row, proj_col, pair_weights):
    rows, ncol = lax.axis_size("row"), lax.axis_size("col")
    span = residues.shape[0]
    window = span * rows
    tile = window // ncol
    width = embed_table.shape[1]
    chans = proj_row.shape[1]
    layers = pair_weights.shape[0]
    kernel = conv_first.shape[0] // width
    half = kernel // 2
    everyone = gather_residues(residues, rows)
    edge = 2 * HALO
    total = span + tile + 4 * edge
    height, wide = span + 2 * HALO, tile + 2 * HALO
    n_pair = height // 2
    two = 2 * chans
    vmem = pl.BlockSpec(memory_space=pltpu.VMEM)
    out = pl.pallas_call(
        functools.partial(main_kernel, (rows, ncol, span, tile, chans, kernel, layers)),
        out_shape=jax.ShapeDtypeStruct((span, chans, tile), BF16),
        in_specs=[vmem] * 7,
        out_specs=vmem,
        scratch_shapes=[
            pltpu.VMEM((32, width), BF16),
            pltpu.VMEM((window + 2 * edge, width), F32),
            pltpu.VMEM((total, width), F32),
            pltpu.VMEM((total - 2 * half, width), F32),
            pltpu.VMEM((total - 2 * half, kernel * width), BF16),
            pltpu.VMEM((height, two), F32),
            pltpu.VMEM((height, two), F32),
            pltpu.VMEM((wide, two), F32),
            pltpu.VMEM((n_pair, wide, two), BF16),
            pltpu.VMEM((n_pair + 2, wide, two), BF16),
            pltpu.VMEM((n_pair + 2, wide, two), BF16),
            pltpu.VMEM((layers, 6 * chans, 6 * chans), BF16),
        ],
        compiler_params=pltpu.CompilerParams(vmem_limit_bytes=48 * 1024 * 1024),
        name="features",
    )(everyone, embed_table, conv_first, conv_second, proj_row, proj_col, pair_weights)
    return jnp.transpose(out, (1, 0, 2))


def solution(mesh):
    return jax.shard_map(
        local,
        mesh=mesh,
        in_specs=(P("row"), P(), P(), P(), P(), P(), P()),
        out_specs=P(None, "row", "col"),
        check_vma=False,
    )
```

```python
import functools

import jax
import jax.numpy as jnp
from jax import lax
from jax.experimental import pallas as pl
from jax.experimental.pallas import tpu as pltpu
from jax.sharding import PartitionSpec as P

MESH = pl.DeviceIdType.MESH
UNROLL = 4
PAD = 4
HALO = 16
F32, BF16 = jnp.float32, jnp.bfloat16


def gather_kernel(n, res_ref, out_ref, buf, send_sem, recv_sem):
    me = lax.axis_index("row")
    barrier = pltpu.get_barrier_semaphore()
    for s in range(1, n):
        pl.semaphore_signal(
            barrier, inc=1, device_id={"row": lax.rem(me + s, n)}, device_id_type=MESH
        )
    pl.semaphore_wait(barrier, n - 1)
    copies = []
    for s in range(1, n):
        copy = pltpu.make_async_remote_copy(
            src_ref=res_ref,
            dst_ref=buf.at[me],
            send_sem=send_sem.at[s],
            recv_sem=recv_sem.at[s],
            device_id={"row": lax.rem(me + s, n)},
            device_id_type=MESH,
        )
        copy.start()
        copies.append(copy)
    for copy in copies:
        copy.wait()
    out_ref[...] = buf[...]
    out_ref[me] = res_ref[...]


def gather_residues(residues, n):
    length = residues.shape[0]
    return pl.pallas_call(
        functools.partial(gather_kernel, n),
        out_shape=jax.ShapeDtypeStruct((n, 1, length), jnp.int32),
        in_specs=[pl.BlockSpec(memory_space=pltpu.VMEM)],
        out_specs=pl.BlockSpec(memory_space=pltpu.VMEM),
        scratch_shapes=[
            pltpu.VMEM((n, 1, length), jnp.int32),
            pltpu.SemaphoreType.DMA((n,)),
            pltpu.SemaphoreType.DMA((n,)),
        ],
        compiler_params=pltpu.CompilerParams(collective_id=0, has_side_effects=True),
        name="gather",
    )(residues.reshape(1, length))


def elu(v):
    return jnp.where(v > 0, v, jnp.exp(jnp.minimum(v, 0.0)) - 1.0)


def main_kernel(
    dims, res_hbm, table_hbm, w1_hbm, w2_hbm, prow_hbm, pcol_hbm, pw_hbm, out_ref,
    res_ref, table_ref, w1_ref, w2_ref, prow_ref, pcol_ref, pw_ref, sems, tab, emb, xs, fs, cols, la, lb, right_ref, pair, act_a, act_b, bw,
):
    rows, ncol, span, tile, chans, kernel, layers = dims
    me_r, me_c = lax.axis_index("row"), lax.axis_index("col")
    window = rows * span
    width = table_ref.shape[1]
    half = kernel // 2
    edge = 2 * HALO
    n_row, n_col = span + 2 * edge, tile + 2 * edge
    height, wide = span + 2 * HALO, tile + 2 * HALO
    two = 2 * chans

    pairs = (
        (pw_hbm, pw_ref), (res_hbm, res_ref), (table_hbm, table_ref), (w1_hbm, w1_ref),
        (w2_hbm, w2_ref), (prow_hbm, prow_ref), (pcol_hbm, pcol_ref),
    )
    loads = [pltpu.make_async_copy(a, b, sems.at[i]) for i, (a, b) in enumerate(pairs)]
    for load in loads:
        load.start()
    loads[0].wait()

    zero = jnp.zeros((chans, chans), BF16)
    for layer in range(layers):
        w = pw_ref[layer].astype(F32).T.astype(BF16)
        for g, offset in enumerate((0, 1, 2, -1)):
            line = []
            for tx in range(3):
                for h in range(2):
                    ty = offset - h + 1
                    tap = 3 * ty + tx
                    here = 0 <= ty <= 2
                    line.append(w[tap * chans : (tap + 1) * chans] if here else zero)
            bw[layer, g * chans : (g + 1) * chans, :] = jnp.concatenate(line, axis=1)

    loads[1].wait()
    loads[2].wait()
    tab[...] = jnp.zeros_like(tab)
    tab[0 : table_ref.shape[0], :] = table_ref[...]
    emb[0:edge, :] = jnp.zeros((edge, width), F32)
    emb[edge + window : 2 * edge + window, :] = jnp.zeros((edge, width), F32)
    per = 128 // span
    vocab = lax.broadcasted_iota(jnp.int32, (tab.shape[0], 128), 0)
    for g in range(window // 128):
        line = jnp.concatenate([res_ref[per * g + m] for m in range(per)], axis=1)
        hot = (jnp.broadcast_to(line, vocab.shape) == vocab).astype(F32).astype(BF16)
        emb[edge + 128 * g : edge + 128 * (g + 1), :] = lax.dot_general(
            hot, tab[...], (((0,), (0,)), ((), ())), preferred_element_type=F32
        )
    xs[0:n_row, :] = emb[pl.ds(pl.multiple_of(me_r * span, span), n_row), :]
    xs[n_row : n_row + n_col, :] = emb[pl.ds(pl.multiple_of(me_c * tile, tile), n_col), :]

    n_first = n_row + n_col - 2 * half
    n_second = n_first - 2 * half
    for k in range(kernel):
        cols[:, k * width : (k + 1) * width] = xs[k : k + n_first, :].astype(BF16)
    loads[3].wait()
    first = elu(jnp.dot(cols[...], w1_ref[...], preferred_element_type=F32))
    at = lax.broadcasted_iota(jnp.int32, (n_first, width), 0) + half
    pos = at + jnp.where(at < n_row, me_r * span - edge, me_c * tile - edge - n_row)
    first = jnp.where((pos >= 0) & (pos < window), first, 0.0)
    fs[...] = first.astype(BF16).astype(F32)
    for k in range(kernel):
        cols[0:n_second, k * width : (k + 1) * width] = fs[k : k + n_second, :].astype(BF16)
    loads[4].wait()
    second = elu(jnp.dot(cols[0:n_second, :], w2_ref[...], preferred_element_type=F32))
    second = (fs[half : half + n_second, :] + second).astype(BF16)

    loads[5].wait()
    loads[6].wait()
    blank = jnp.zeros((chans, width), BF16)
    pr, pc = prow_ref[...], pcol_ref[...]
    s_row, s_col = second[0:height], second[n_row : n_row + wide]
    dot = functools.partial(jnp.dot, preferred_element_type=F32)

    def project(x, *parts):
        w = jnp.concatenate(parts, axis=0)
        y = lax.dot_general(x, w, (((1,), (1,)), ((), ())), preferred_element_type=F32)
        return y.astype(BF16).astype(F32)

    la[...] = project(s_row, pr, blank)
    lb[...] = project(s_row, blank, pr)
    right_ref[...] = project(s_col, pc, pc)
    n_pair = height // 2
    blank_pair = jnp.zeros((PAD, wide, two), BF16)
    for act in (act_a, act_b):
        act[0:PAD] = blank_pair
        act[PAD + n_pair : 2 * PAD + n_pair] = blank_pair

    def mask(act):
        side = jnp.zeros((HALO // 2, wide, two), BF16)
        stripe = jnp.zeros((n_pair + 2 * PAD, HALO, two), BF16)

        @pl.when(me_r == 0)
        def _():
            act[PAD : PAD + HALO // 2] = side

        @pl.when(me_r == rows - 1)
        def _():
            act[PAD + n_pair - HALO // 2 : PAD + n_pair] = side

        @pl.when(me_c == 0)
        def _():
            act[:, 0:HALO, :] = stripe

        @pl.when(me_c == ncol - 1)
        def _():
            act[:, wide - HALO : wide, :] = stripe

    def start(p, _):
        left = la[pl.ds(2 * p, 1), :] + lb[pl.ds(2 * p + 1, 1), :]
        value = (right_ref[...] + left).astype(BF16)
        pair[p] = value
        act_a[p + PAD] = elu(value.astype(F32)).astype(BF16)
        return 0

    lax.fori_loop(0, n_pair, start, 0)
    mask(act_a)

    low_half = lax.broadcasted_iota(jnp.int32, (wide, two), 1) < chans
    bufs = (act_a, act_b)
    for layer in range(layers):
        src, dst = bufs[layer % 2], bufs[(layer + 1) % 2]
        d = 2**layer
        last = layer == layers - 1

        def step(q, _, layer=layer, src=src, dst=dst, d=d, last=last):
            if last:
                slots = [HALO // 2 + 2 * q, HALO // 2 + 2 * q + 1]
            else:
                x = 2 * d * lax.div(q, d) + lax.rem(q, d)
                slots = [x, x + d]
            lhs = jnp.concatenate(
                [
                    jnp.concatenate(
                        [
                            src[p + PAD],
                            jnp.where(low_half, src[p + PAD + d], src[p + PAD - d]),
                        ],
                        axis=1,
                    )
                    for p in slots
                ],
                axis=0,
            )
            got = dot(lhs, bw[layer])
            low = pltpu.roll(got[:, 0:two], d, 0)
            mid = got[:, two : 2 * two]
            high = pltpu.roll(got[:, 2 * two : 3 * two], 2 * wide - d, 0)
            total = low + mid + high
            values = [
                pair[p].astype(F32) + total[k * wide : (k + 1) * wide]
                for k, p in enumerate(slots)
            ]
            if last:
                for p, value in zip(slots, values):
                    turned = value[HALO : HALO + tile].T.astype(BF16)
                    at = p - HALO // 2
                    line = 2 * d * lax.div(at, d) + lax.rem(at, d)
                    out_ref[line] = turned[0:chans]
                    out_ref[line + d] = turned[chans:two]
            else:
                one, other = (v.astype(BF16) for v in values)
                new = [
                    jnp.where(low_half, one, pltpu.roll(other, chans, 1)),
                    jnp.where(low_half, pltpu.roll(one, chans, 1), other),
                ]
                for p, value in zip(slots, new):
                    pair[p] = value
                    dst[p + PAD] = elu(value.astype(F32)).astype(BF16)
            return 0

        steps = (n_pair - HALO) // 2 if last else n_pair // 2
        lax.fori_loop(0, steps, step, 0, unroll=UNROLL)
        if not last:
            mask(dst)


def local(residues, embed_table, conv_first, conv_second, proj_row, proj_col, pair_weights):
    rows, ncol = lax.axis_size("row"), lax.axis_size("col")
    span = residues.shape[0]
    window = span * rows
    tile = window // ncol
    width = embed_table.shape[1]
    chans = proj_row.shape[1]
    layers = pair_weights.shape[0]
    kernel = conv_first.shape[0] // width
    half = kernel // 2
    everyone = gather_residues(residues, rows)
    edge = 2 * HALO
    total = span + tile + 4 * edge
    height, wide = span + 2 * HALO, tile + 2 * HALO
    n_pair = height // 2
    two = 2 * chans
    vmem = pl.BlockSpec(memory_space=pltpu.VMEM)
    out = pl.pallas_call(
        functools.partial(main_kernel, (rows, ncol, span, tile, chans, kernel, layers)),
        out_shape=jax.ShapeDtypeStruct((span, chans, tile), BF16),
        in_specs=[pl.BlockSpec(memory_space=pltpu.HBM)] * 7,
        out_specs=vmem,
        scratch_shapes=[
            pltpu.VMEM(everyone.shape, jnp.int32),
            pltpu.VMEM(embed_table.shape, BF16),
            pltpu.VMEM(conv_first.shape, BF16),
            pltpu.VMEM(conv_second.shape, BF16),
            pltpu.VMEM((chans, width), BF16),
            pltpu.VMEM((chans, width), BF16),
            pltpu.VMEM(pair_weights.shape, BF16),
            pltpu.SemaphoreType.DMA((7,)),
            pltpu.VMEM((32, width), BF16),
            pltpu.VMEM((window + 2 * edge, width), F32),
            pltpu.VMEM((total, width), F32),
            pltpu.VMEM((total - 2 * half, width), F32),
            pltpu.VMEM((total - 2 * half, kernel * width), BF16),
            pltpu.VMEM((height, two), F32),
            pltpu.VMEM((height, two), F32),
            pltpu.VMEM((wide, two), F32),
            pltpu.VMEM((n_pair, wide, two), BF16),
            pltpu.VMEM((n_pair + 2 * PAD, wide, two), BF16),
            pltpu.VMEM((n_pair + 2 * PAD, wide, two), BF16),
            pltpu.VMEM((layers, 4 * chans, 6 * chans), BF16),
        ],
        compiler_params=pltpu.CompilerParams(vmem_limit_bytes=60 * 1024 * 1024),
        name="features",
    )(everyone, embed_table, conv_first, conv_second, proj_row.T, proj_col.T, pair_weights)
    return jnp.transpose(out, (1, 0, 2))


def solution(mesh):
    return jax.shard_map(
        local,
        mesh=mesh,
        in_specs=(P("row"), P(), P(), P(), P(), P(), P()),
        out_specs=P(None, "row", "col"),
        check_vma=False,
    )
```

```python
import functools

import jax
import jax.numpy as jnp
from jax import lax
from jax.experimental import pallas as pl
from jax.experimental.pallas import tpu as pltpu
from jax.sharding import PartitionSpec as P

MESH = pl.DeviceIdType.MESH
UNROLL = 8
PAD = 4
HALO = 16
F32, BF16 = jnp.float32, jnp.bfloat16


def elu(v):
    return jnp.where(v > 0, v, jnp.exp(jnp.minimum(v, 0.0)) - 1.0)


def main_kernel(
    dims, res_hbm, table_hbm, w1_hbm, w2_hbm, prow_hbm, pcol_hbm, pw_hbm, out_ref,
    res_ref, table_ref, w1_ref, w2_ref, prow_ref, pcol_ref, pw_ref, sems, send_sem, recv_sem, tab, emb, xs, fs, cols, la, lb, right_ref, pair, act_a, act_b, bw,
):
    rows, ncol, span, tile, chans, kernel, layers = dims
    me_r, me_c = lax.axis_index("row"), lax.axis_index("col")
    window = rows * span
    width = table_ref.shape[1]
    half = kernel // 2
    edge = 2 * HALO
    n_row, n_col = span + 2 * edge, tile + 2 * edge
    height, wide = span + 2 * HALO, tile + 2 * HALO
    two = 2 * chans

    barrier = pltpu.get_barrier_semaphore()
    for k in range(1, rows):
        pl.semaphore_signal(
            barrier, inc=1, device_id={"row": lax.rem(me_r + k, rows)}, device_id_type=MESH
        )
    pairs = (
        (pw_hbm, pw_ref), (res_hbm, res_ref.at[me_r]), (table_hbm, table_ref), (w1_hbm, w1_ref),
        (w2_hbm, w2_ref), (prow_hbm, prow_ref), (pcol_hbm, pcol_ref),
    )
    loads = [pltpu.make_async_copy(a, b, sems.at[i]) for i, (a, b) in enumerate(pairs)]
    for load in loads:
        load.start()
    loads[0].wait()

    zero = jnp.zeros((chans, chans), BF16)
    for layer in range(layers):
        w = pw_ref[layer].astype(F32).T.astype(BF16)
        for g, offset in enumerate((0, 1, 2, -1)):
            line = []
            for tx in range(3):
                for h in range(2):
                    ty = offset - h + 1
                    tap = 3 * ty + tx
                    here = 0 <= ty <= 2
                    line.append(w[tap * chans : (tap + 1) * chans] if here else zero)
            bw[layer, g * chans : (g + 1) * chans, :] = jnp.concatenate(line, axis=1)
    n_pair = height // 2
    blank_pair = jnp.zeros((PAD, wide, two), BF16)
    for act in (act_a, act_b):
        act[0:PAD] = blank_pair
        act[PAD + n_pair : 2 * PAD + n_pair] = blank_pair

    pl.semaphore_wait(barrier, rows - 1)
    copies = [
        pltpu.make_async_remote_copy(
            src_ref=res_hbm,
            dst_ref=res_ref.at[me_r],
            send_sem=send_sem.at[k],
            recv_sem=recv_sem.at[k],
            device_id={"row": lax.rem(me_r + k, rows)},
            device_id_type=MESH,
        )
        for k in range(1, rows)
    ]
    for copy in copies:
        copy.start()

    loads[2].wait()
    tab[...] = jnp.zeros_like(tab)
    tab[0 : table_ref.shape[0], :] = table_ref[...]
    emb[0:edge, :] = jnp.zeros((edge, width), F32)
    emb[edge + window : 2 * edge + window, :] = jnp.zeros((edge, width), F32)
    loads[1].wait()
    for copy in copies:
        copy.wait()
    per = 128 // span
    vocab = lax.broadcasted_iota(jnp.int32, (tab.shape[0], 128), 0)
    for g in range(window // 128):
        line = jnp.concatenate([res_ref[per * g + m] for m in range(per)], axis=1)
        hot = (jnp.broadcast_to(line, vocab.shape) == vocab).astype(F32).astype(BF16)
        emb[edge + 128 * g : edge + 128 * (g + 1), :] = lax.dot_general(
            hot, tab[...], (((0,), (0,)), ((), ())), preferred_element_type=F32
        )
    xs[0:n_row, :] = emb[pl.ds(pl.multiple_of(me_r * span, span), n_row), :]
    xs[n_row : n_row + n_col, :] = emb[pl.ds(pl.multiple_of(me_c * tile, tile), n_col), :]

    n_first = n_row + n_col - 2 * half
    n_second = n_first - 2 * half
    for k in range(kernel):
        cols[:, k * width : (k + 1) * width] = xs[k : k + n_first, :].astype(BF16)
    loads[3].wait()
    first = elu(jnp.dot(cols[...], w1_ref[...], preferred_element_type=F32))
    at = lax.broadcasted_iota(jnp.int32, (n_first, width), 0) + half
    pos = at + jnp.where(at < n_row, me_r * span - edge, me_c * tile - edge - n_row)
    first = jnp.where((pos >= 0) & (pos < window), first, 0.0)
    fs[...] = first.astype(BF16).astype(F32)
    for k in range(kernel):
        cols[0:n_second, k * width : (k + 1) * width] = fs[k : k + n_second, :].astype(BF16)
    loads[4].wait()
    second = elu(jnp.dot(cols[0:n_second, :], w2_ref[...], preferred_element_type=F32))
    second = (fs[half : half + n_second, :] + second).astype(BF16)

    loads[5].wait()
    loads[6].wait()
    blank = jnp.zeros((chans, width), BF16)
    pr, pc = prow_ref[...], pcol_ref[...]
    s_row, s_col = second[0:height], second[n_row : n_row + wide]
    dot = functools.partial(jnp.dot, preferred_element_type=F32)

    def project(x, *parts):
        w = jnp.concatenate(parts, axis=0)
        y = lax.dot_general(x, w, (((1,), (1,)), ((), ())), preferred_element_type=F32)
        return y.astype(BF16).astype(F32)

    la[...] = project(s_row, pr, blank)
    lb[...] = project(s_row, blank, pr)
    right_ref[...] = project(s_col, pc, pc)

    def mask(act):
        side = jnp.zeros((HALO // 2, wide, two), BF16)
        stripe = jnp.zeros((n_pair + 2 * PAD, HALO, two), BF16)

        @pl.when(me_r == 0)
        def _():
            act[PAD : PAD + HALO // 2] = side

        @pl.when(me_r == rows - 1)
        def _():
            act[PAD + n_pair - HALO // 2 : PAD + n_pair] = side

        @pl.when(me_c == 0)
        def _():
            act[:, 0:HALO, :] = stripe

        @pl.when(me_c == ncol - 1)
        def _():
            act[:, wide - HALO : wide, :] = stripe

    def start(p, _):
        left = la[pl.ds(2 * p, 1), :] + lb[pl.ds(2 * p + 1, 1), :]
        value = (right_ref[...] + left).astype(BF16)
        pair[p] = value
        act_a[p + PAD] = elu(value.astype(F32)).astype(BF16)
        return 0

    lax.fori_loop(0, n_pair, start, 0)
    mask(act_a)

    low_half = lax.broadcasted_iota(jnp.int32, (wide, two), 1) < chans
    bufs = (act_a, act_b)
    for layer in range(layers):
        src, dst = bufs[layer % 2], bufs[(layer + 1) % 2]
        d = 2**layer
        last = layer == layers - 1

        def step(q, _, layer=layer, src=src, dst=dst, d=d, last=last):
            if last:
                slots = [HALO // 2 + 2 * q, HALO // 2 + 2 * q + 1]
            else:
                x = 2 * d * lax.div(q, d) + lax.rem(q, d)
                slots = [x, x + d]
            lhs = jnp.concatenate(
                [
                    jnp.concatenate(
                        [
                            src[p + PAD],
                            jnp.where(low_half, src[p + PAD + d], src[p + PAD - d]),
                        ],
                        axis=1,
                    )
                    for p in slots
                ],
                axis=0,
            )
            got = dot(lhs, bw[layer])
            low = pltpu.roll(got[:, 0:two], d, 0)
            mid = got[:, two : 2 * two]
            high = pltpu.roll(got[:, 2 * two : 3 * two], 2 * wide - d, 0)
            total = low + mid + high
            values = [
                pair[p].astype(F32) + total[k * wide : (k + 1) * wide]
                for k, p in enumerate(slots)
            ]
            if last:
                for p, value in zip(slots, values):
                    turned = value[HALO : HALO + tile].T.astype(BF16)
                    at = p - HALO // 2
                    line = 2 * d * lax.div(at, d) + lax.rem(at, d)
                    out_ref[line] = turned[0:chans]
                    out_ref[line + d] = turned[chans:two]
            else:
                one, other = (v.astype(BF16) for v in values)
                new = [
                    jnp.where(low_half, one, pltpu.roll(other, chans, 1)),
                    jnp.where(low_half, pltpu.roll(one, chans, 1), other),
                ]
                for p, value in zip(slots, new):
                    pair[p] = value
                    dst[p + PAD] = elu(value.astype(F32)).astype(BF16)
            return 0

        steps = (n_pair - HALO) // 2 if last else n_pair // 2
        lax.fori_loop(0, steps, step, 0, unroll=UNROLL)
        if not last:
            mask(dst)


def local(residues, embed_table, conv_first, conv_second, proj_row, proj_col, pair_weights):
    rows, ncol = lax.axis_size("row"), lax.axis_size("col")
    span = residues.shape[0]
    window = span * rows
    tile = window // ncol
    width = embed_table.shape[1]
    chans = proj_row.shape[1]
    layers = pair_weights.shape[0]
    kernel = conv_first.shape[0] // width
    half = kernel // 2
    edge = 2 * HALO
    total = span + tile + 4 * edge
    height, wide = span + 2 * HALO, tile + 2 * HALO
    n_pair = height // 2
    two = 2 * chans
    vmem = pl.BlockSpec(memory_space=pltpu.VMEM)
    out = pl.pallas_call(
        functools.partial(main_kernel, (rows, ncol, span, tile, chans, kernel, layers)),
        out_shape=jax.ShapeDtypeStruct((span, chans, tile), BF16),
        in_specs=[pl.BlockSpec(memory_space=pltpu.HBM)] * 7,
        out_specs=vmem,
        scratch_shapes=[
            pltpu.VMEM((rows, 1, span), jnp.int32),
            pltpu.VMEM(embed_table.shape, BF16),
            pltpu.VMEM(conv_first.shape, BF16),
            pltpu.VMEM(conv_second.shape, BF16),
            pltpu.VMEM((chans, width), BF16),
            pltpu.VMEM((chans, width), BF16),
            pltpu.VMEM(pair_weights.shape, BF16),
            pltpu.SemaphoreType.DMA((7,)),
            pltpu.SemaphoreType.DMA((rows,)),
            pltpu.SemaphoreType.DMA((rows,)),
            pltpu.VMEM((32, width), BF16),
            pltpu.VMEM((window + 2 * edge, width), F32),
            pltpu.VMEM((total, width), F32),
            pltpu.VMEM((total - 2 * half, width), F32),
            pltpu.VMEM((total - 2 * half, kernel * width), BF16),
            pltpu.VMEM((height, two), F32),
            pltpu.VMEM((height, two), F32),
            pltpu.VMEM((wide, two), F32),
            pltpu.VMEM((n_pair, wide, two), BF16),
            pltpu.VMEM((n_pair + 2 * PAD, wide, two), BF16),
            pltpu.VMEM((n_pair + 2 * PAD, wide, two), BF16),
            pltpu.VMEM((layers, 4 * chans, 6 * chans), BF16),
        ],
        compiler_params=pltpu.CompilerParams(
            vmem_limit_bytes=60 * 1024 * 1024, collective_id=0, has_side_effects=True
        ),
        name="all",
    )(residues.reshape(1, span), embed_table, conv_first, conv_second, proj_row.T, proj_col.T, pair_weights)
    return jnp.transpose(out, (1, 0, 2))


def solution(mesh):
    return jax.shard_map(
        local,
        mesh=mesh,
        in_specs=(P("row"), P(), P(), P(), P(), P(), P()),
        out_specs=P(None, "row", "col"),
        check_vma=False,
    )
```

```python
import functools

import jax
import jax.numpy as jnp
from jax import lax
from jax.experimental import pallas as pl
from jax.experimental.pallas import tpu as pltpu
from jax.sharding import PartitionSpec as P

MESH = pl.DeviceIdType.MESH
UNROLL = 8
PAD = 4
HALO = 16
F32, BF16 = jnp.float32, jnp.bfloat16


def elu(v):
    return jnp.where(v > 0, v, jnp.exp(jnp.minimum(v, 0.0)) - 1.0)


def main_kernel(
    dims, res_hbm, table_hbm, w1_hbm, w2_hbm, prow_hbm, pcol_hbm, pw_hbm, out_ref,
    res_ref, table_ref, w1_ref, w2_ref, prow_ref, pcol_ref, pw_ref, sems, send_sem, recv_sem, tab, emb, xs, fs, cols, la, lb, right_ref, pair, act_a, act_b, bw,
):
    rows, ncol, span, tile, chans, kernel, layers = dims
    me_r, me_c = lax.axis_index("row"), lax.axis_index("col")
    window = rows * span
    width = table_ref.shape[1]
    half = kernel // 2
    edge = 2 * HALO
    n_row, n_col = span + 2 * edge, tile + 2 * edge
    height, wide = span + 2 * HALO, tile + 2 * HALO
    two = 2 * chans

    barrier = pltpu.get_barrier_semaphore()
    for k in range(1, rows):
        pl.semaphore_signal(
            barrier, inc=1, device_id={"row": lax.rem(me_r + k, rows)}, device_id_type=MESH
        )
    pairs = (
        (pw_hbm, pw_ref), (res_hbm, res_ref.at[me_r]), (table_hbm, table_ref), (w1_hbm, w1_ref),
        (w2_hbm, w2_ref), (prow_hbm, prow_ref), (pcol_hbm, pcol_ref),
    )
    loads = [pltpu.make_async_copy(a, b, sems.at[i]) for i, (a, b) in enumerate(pairs)]
    for load in loads:
        load.start()
    loads[0].wait()

    zero = jnp.zeros((chans, chans), BF16)
    for layer in range(layers):
        w = pw_ref[layer].astype(F32).T.astype(BF16)
        for g, offset in enumerate((0, 1, 2, -1)):
            line = []
            for tx in range(3):
                for h in range(2):
                    ty = offset - h + 1
                    tap = 3 * ty + tx
                    here = 0 <= ty <= 2
                    line.append(w[tap * chans : (tap + 1) * chans] if here else zero)
            bw[layer, g * chans : (g + 1) * chans, :] = jnp.concatenate(line, axis=1)
    n_pair = height // 2
    blank_pair = jnp.zeros((PAD, wide, two), BF16)
    for act in (act_a, act_b):
        act[0:PAD] = blank_pair
        act[PAD + n_pair : 2 * PAD + n_pair] = blank_pair

    pl.semaphore_wait(barrier, rows - 1)
    copies = [
        pltpu.make_async_remote_copy(
            src_ref=res_hbm,
            dst_ref=res_ref.at[me_r],
            send_sem=send_sem.at[k],
            recv_sem=recv_sem.at[k],
            device_id={"row": lax.rem(me_r + k, rows)},
            device_id_type=MESH,
        )
        for k in range(1, rows)
    ]
    for copy in copies:
        copy.start()

    loads[2].wait()
    tab[...] = jnp.zeros_like(tab)
    tab[0 : table_ref.shape[0], :] = table_ref[...]
    emb[0:edge, :] = jnp.zeros((edge, width), F32)
    emb[edge + window : 2 * edge + window, :] = jnp.zeros((edge, width), F32)
    loads[1].wait()
    for copy in copies:
        copy.wait()
    per = 128 // span
    vocab = lax.broadcasted_iota(jnp.int32, (tab.shape[0], 128), 0)
    for g in range(window // 128):
        line = jnp.concatenate([res_ref[per * g + m] for m in range(per)], axis=1)
        hot = (jnp.broadcast_to(line, vocab.shape) == vocab).astype(F32).astype(BF16)
        emb[edge + 128 * g : edge + 128 * (g + 1), :] = lax.dot_general(
            hot, tab[...], (((0,), (0,)), ((), ())), preferred_element_type=F32
        )
    xs[0:n_row, :] = emb[pl.ds(pl.multiple_of(me_r * span, span), n_row), :]
    xs[n_row : n_row + n_col, :] = emb[pl.ds(pl.multiple_of(me_c * tile, tile), n_col), :]

    n_first = n_row + n_col - 2 * half
    n_second = n_first - 2 * half
    for k in range(kernel):
        cols[:, k * width : (k + 1) * width] = xs[k : k + n_first, :].astype(BF16)
    loads[3].wait()
    first = elu(jnp.dot(cols[...], w1_ref[...], preferred_element_type=F32))
    at = lax.broadcasted_iota(jnp.int32, (n_first, width), 0) + half
    pos = at + jnp.where(at < n_row, me_r * span - edge, me_c * tile - edge - n_row)
    first = jnp.where((pos >= 0) & (pos < window), first, 0.0)
    fs[...] = first.astype(BF16).astype(F32)
    for k in range(kernel):
        cols[0:n_second, k * width : (k + 1) * width] = fs[k : k + n_second, :].astype(BF16)
    loads[4].wait()
    second = elu(jnp.dot(cols[0:n_second, :], w2_ref[...], preferred_element_type=F32))
    second = (fs[half : half + n_second, :] + second).astype(BF16)

    loads[5].wait()
    loads[6].wait()
    blank = jnp.zeros((chans, width), BF16)
    pr, pc = prow_ref[...], pcol_ref[...]
    s_row, s_col = second[0:height], second[n_row : n_row + wide]
    dot = functools.partial(jnp.dot, preferred_element_type=F32)

    def project(x, *parts):
        w = jnp.concatenate(parts, axis=0)
        y = lax.dot_general(x, w, (((1,), (1,)), ((), ())), preferred_element_type=F32)
        return y.astype(BF16).astype(F32)

    la[...] = project(s_row, pr, blank)
    lb[...] = project(s_row, blank, pr)
    right_ref[...] = project(s_col, pc, pc)

    def mask(act):
        side = jnp.zeros((HALO // 2, wide, two), BF16)
        stripe = jnp.zeros((n_pair + 2 * PAD, HALO, two), BF16)

        @pl.when(me_r == 0)
        def _():
            act[PAD : PAD + HALO // 2] = side

        @pl.when(me_r == rows - 1)
        def _():
            act[PAD + n_pair - HALO // 2 : PAD + n_pair] = side

        @pl.when(me_c == 0)
        def _():
            act[:, 0:HALO, :] = stripe

        @pl.when(me_c == ncol - 1)
        def _():
            act[:, wide - HALO : wide, :] = stripe

    def start(p, _):
        left = la[pl.ds(2 * p, 1), :] + lb[pl.ds(2 * p + 1, 1), :]
        value = (right_ref[...] + left).astype(BF16)
        pair[p] = value
        act_a[p + PAD] = elu(value.astype(F32)).astype(BF16)
        return 0

    lax.fori_loop(0, n_pair, start, 0, unroll=4)
    mask(act_a)

    low_half = lax.broadcasted_iota(jnp.int32, (wide, two), 1) < chans
    bufs = (act_a, act_b)
    for layer in range(layers):
        src, dst = bufs[layer % 2], bufs[(layer + 1) % 2]
        d = 2**layer
        last = layer == layers - 1

        def step(q, _, layer=layer, src=src, dst=dst, d=d, last=last, rim=False):
            if last:
                slots = [HALO // 2 + 2 * q, HALO // 2 + 2 * q + 1]
            elif rim:
                slots = [q + d, n_pair - 2 * d + q]
            else:
                x = 2 * d * lax.div(q, d) + lax.rem(q, d)
                slots = [x, x + d]
            lhs = jnp.concatenate(
                [
                    jnp.concatenate(
                        [
                            src[p + PAD],
                            jnp.where(low_half, src[p + PAD + d], src[p + PAD - d]),
                        ],
                        axis=1,
                    )
                    for p in slots
                ],
                axis=0,
            )
            got = dot(lhs, bw[layer])
            low = pltpu.roll(got[:, 0:two], d, 0)
            mid = got[:, two : 2 * two]
            high = pltpu.roll(got[:, 2 * two : 3 * two], 2 * wide - d, 0)
            total = low + mid + high
            values = [
                pair[p].astype(F32) + total[k * wide : (k + 1) * wide]
                for k, p in enumerate(slots)
            ]
            if last:
                for p, value in zip(slots, values):
                    turned = value[HALO : HALO + tile].T.astype(BF16)
                    at = p - HALO // 2
                    line = 2 * d * lax.div(at, d) + lax.rem(at, d)
                    out_ref[line] = turned[0:chans]
                    out_ref[line + d] = turned[chans:two]
            else:
                one, other = (v.astype(BF16) for v in values)
                if rim:
                    first_pair, last_pair = one, other
                    new = [
                        pltpu.roll(first_pair, chans, 1), first_pair,
                        last_pair, pltpu.roll(last_pair, chans, 1),
                    ]
                    slots = [q, q + d, n_pair - 2 * d + q, n_pair - d + q]
                else:
                    new = [
                        jnp.where(low_half, one, pltpu.roll(other, chans, 1)),
                        jnp.where(low_half, pltpu.roll(one, chans, 1), other),
                    ]
                for p, value in zip(slots, new):
                    pair[p] = value
                    dst[p + PAD] = elu(value.astype(F32)).astype(BF16)
            return 0

        if last:
            lax.fori_loop(0, (n_pair - HALO) // 2, step, 0, unroll=UNROLL)
        else:
            lax.fori_loop(0, d, functools.partial(step, rim=True), 0, unroll=d)
            lax.fori_loop(d, n_pair // 2 - d, step, 0, unroll=UNROLL)
        if not last:
            mask(dst)


def local(residues, embed_table, conv_first, conv_second, proj_row, proj_col, pair_weights):
    rows, ncol = lax.axis_size("row"), lax.axis_size("col")
    span = residues.shape[0]
    window = span * rows
    tile = window // ncol
    width = embed_table.shape[1]
    chans = proj_row.shape[1]
    layers = pair_weights.shape[0]
    kernel = conv_first.shape[0] // width
    half = kernel // 2
    edge = 2 * HALO
    total = span + tile + 4 * edge
    height, wide = span + 2 * HALO, tile + 2 * HALO
    n_pair = height // 2
    two = 2 * chans
    vmem = pl.BlockSpec(memory_space=pltpu.VMEM)
    out = pl.pallas_call(
        functools.partial(main_kernel, (rows, ncol, span, tile, chans, kernel, layers)),
        out_shape=jax.ShapeDtypeStruct((span, chans, tile), BF16),
        in_specs=[pl.BlockSpec(memory_space=pltpu.HBM)] * 7,
        out_specs=vmem,
        scratch_shapes=[
            pltpu.VMEM((rows, 1, span), jnp.int32),
            pltpu.VMEM(embed_table.shape, BF16),
            pltpu.VMEM(conv_first.shape, BF16),
            pltpu.VMEM(conv_second.shape, BF16),
            pltpu.VMEM((chans, width), BF16),
            pltpu.VMEM((chans, width), BF16),
            pltpu.VMEM(pair_weights.shape, BF16),
            pltpu.SemaphoreType.DMA((7,)),
            pltpu.SemaphoreType.DMA((rows,)),
            pltpu.SemaphoreType.DMA((rows,)),
            pltpu.VMEM((32, width), BF16),
            pltpu.VMEM((window + 2 * edge, width), F32),
            pltpu.VMEM((total, width), F32),
            pltpu.VMEM((total - 2 * half, width), F32),
            pltpu.VMEM((total - 2 * half, kernel * width), BF16),
            pltpu.VMEM((height, two), F32),
            pltpu.VMEM((height, two), F32),
            pltpu.VMEM((wide, two), F32),
            pltpu.VMEM((n_pair, wide, two), BF16),
            pltpu.VMEM((n_pair + 2 * PAD, wide, two), BF16),
            pltpu.VMEM((n_pair + 2 * PAD, wide, two), BF16),
            pltpu.VMEM((layers, 4 * chans, 6 * chans), BF16),
        ],
        compiler_params=pltpu.CompilerParams(
            vmem_limit_bytes=60 * 1024 * 1024, collective_id=0, has_side_effects=True
        ),
        name="all",
    )(residues.reshape(1, span), embed_table, conv_first, conv_second, proj_row.T, proj_col.T, pair_weights)
    return jnp.transpose(out, (1, 0, 2))


def solution(mesh):
    return jax.shard_map(
        local,
        mesh=mesh,
        in_specs=(P("row"), P(), P(), P(), P(), P(), P()),
        out_specs=P(None, "row", "col"),
        check_vma=False,
    )
```
